1024 devices in a mesh: ctx: 32 (over y, z_lo), fsdp: 32 (over z_hi, x, core).
Axes of the slice: x: 4, y: 8, z: 16 (z_hi: 4, z_lo: 4; z = z_hi * 4 + z_lo), core: 2. Of those that a mesh axis runs over, the one named last changes fastest.
Arguments:
- grad_out: bfloat16 [4096, 8192], P('ctx', 'fsdp'), may hold values from -6 to 6
- queries: bfloat16 [4096, 8192], P('ctx', 'fsdp'), may hold values from -6 to 6
- keys_in: bfloat16 [4096, 8192], P('ctx', 'fsdp'), may hold values from -6 to 6
- values_in: bfloat16 [4096, 8192], P('ctx', 'fsdp'), may hold values from -6 to 6
- filters: bfloat16 [512, 128], P('fsdp'), may hold values from -1.25 to 1.25
- out_weight: bfloat16 [8192, 8192], P('ctx', 'fsdp'), may hold values from -0.0625 to 0.0625
Outputs:
- grad_q: bfloat16 [4096, 8192], P('ctx', 'fsdp')
- grad_k: bfloat16 [4096, 8192], P('ctx', 'fsdp')
- grad_v: bfloat16 [4096, 8192], P('ctx', 'fsdp')
- grad_filters: float32 [512, 128], P('fsdp')
The draws below stay inside these ranges and needn't reach their ends.
All inputs are finite; a program needn't handle non-finite values.
Results may differ from the reference program's by a relative error of at most 0.015.
Values may be sent and summed in bfloat16 or wider, within the bound.
A program may use at most 32 MiB of HBM per device.

```python
import jax
import jax.numpy as jnp
from jax import lax

D = 8192
G = 512
TAPS = 128
TOKENS = 4096


def block_levels(key, extent, split, least, top_value):
    def one(dim, parts):
        steps = jax.random.uniform(jax.random.fold_in(jax.random.fold_in(key, 6), dim), (parts,), jnp.float32, least / len(split), top_value / len(split))
        return jnp.repeat(jnp.exp(steps), extent[dim] // parts).reshape((-1,) + (1,) * (len(extent) - dim - 1))

    level = one(*split[0])
    for cut in split[1:]:
        level = level * one(*cut)
    return level


def normal_values(stream_key, dims, spread, bound, pieces=(), kind=jnp.bfloat16):
    array = spread * jax.random.normal(stream_key, dims, jnp.float32)
    if pieces:
        array = array * block_levels(stream_key, dims, pieces, -0.22, 0.18)
    return jnp.clip(array, -bound, bound).astype(kind)


def setup_inputs(seed: int = 0) -> dict:
    seeds = jax.random.split(jax.random.key(seed), 7)
    return {
        "grad_out": normal_values(seeds[0], (TOKENS, D), 1.0, 6.0, ((0, 32), (1, 32))),
        "queries": normal_values(seeds[1], (TOKENS, D), 1.0, 6.0, ((0, 32), (1, 32))),
        "keys_in": normal_values(seeds[2], (TOKENS, D), 1.0, 6.0, ((0, 32), (1, 32))),
        "values_in": normal_values(seeds[3], (TOKENS, D), 1.0, 6.0, ((0, 32), (1, 32))),
        "filters": normal_values(seeds[4], (G, TAPS), 0.09, 1.25, ((0, 32),)),
        "out_weight": normal_values(seeds[5], (D, D), D ** -0.5, 0.0625, ((0, 32), (1, 32))),
    }


def reference(grad_out, queries, keys_in, values_in, filters, out_weight):
    grad_y = jnp.dot(grad_out, out_weight, preferred_element_type=jnp.float32).astype(jnp.bfloat16)
    kvp = (keys_in.astype(jnp.float32) * values_in.astype(jnp.float32)).astype(jnp.bfloat16)
    kv_float = kvp.astype(jnp.float32)
    length = kv_float.shape[0]
    width = kv_float.shape[1]
    groups = filters.shape[0]
    taps = filters.shape[1]
    per_group = width // groups
    chan_filter = jnp.repeat(filters.astype(jnp.float32), per_group, axis=0).T
    kv_padded = jnp.concatenate([jnp.zeros((taps - 1, width), jnp.float32), kv_float], axis=0)

    def forward_tap(j, total):
        row = lax.dynamic_slice_in_dim(chan_filter, j, 1, 0)
        piece = lax.dynamic_slice_in_dim(kv_padded, taps - 1 - j, length, 0)
        return total + row * piece

    z_conv = lax.fori_loop(0, taps, forward_tap, jnp.zeros((length, width), jnp.float32))
    grad_yf = grad_y.astype(jnp.float32)
    grad_q = (grad_yf * z_conv).astype(jnp.bfloat16)
    grad_z = (grad_yf * queries.astype(jnp.float32)).astype(jnp.bfloat16)
    grad_zf = grad_z.astype(jnp.float32)
    gz_padded = jnp.concatenate([grad_zf, jnp.zeros((taps - 1, width), jnp.float32)], axis=0)

    def backward_tap(j, carry):
        total, rows = carry
        row = lax.dynamic_slice_in_dim(chan_filter, j, 1, 0)
        piece = lax.dynamic_slice_in_dim(gz_padded, j, length, 0)
        total = total + row * piece
        shifted = lax.dynamic_slice_in_dim(kv_padded, taps - 1 - j, length, 0)
        per_chan = jnp.sum(grad_zf * shifted, axis=0)
        per_group_sum = jnp.sum(per_chan.reshape(groups, per_group), axis=1)
        rows = lax.dynamic_update_slice_in_dim(rows, per_group_sum[None, :], j, 0)
        return total, rows

    grad_kv, filter_rows = lax.fori_loop(0, taps, backward_tap, (jnp.zeros((length, width), jnp.float32), jnp.zeros((taps, groups), jnp.float32)))
    grad_k = (grad_kv * values_in.astype(jnp.float32)).astype(jnp.bfloat16)
    grad_v = (grad_kv * keys_in.astype(jnp.float32)).astype(jnp.bfloat16)
    return grad_q, grad_k, grad_v, filter_rows.T
```

```python
import jax
import jax.numpy as jnp
from jax import lax
from jax.experimental import pallas as pl
from jax.experimental.pallas import tpu as pltpu
from jax.sharding import PartitionSpec as P

MESH = pl.DeviceIdType.MESH
NX, NY, NH, NL = 4, 8, 4, 4
NZ = NH * NL
ROWS = 128
WIDE = 256
HALF = 64
GROUPS = 16
TAPS = 128
F32, BF16 = jnp.float32, jnp.bfloat16


def mod(value, size):
    return lax.rem(value + size, size)


def kernel(
    go, queries, keys, values, filters, weight,
    out_q, out_k, out_v, out_f,
    grads, rows_w, staged, part, part_in, kvx, kvrev, gzx, toe_z, toe_b, conv, sums_l, sums_y,
    w_send, w_recv, pre_send, pre_recv, z1_send, z2_send, z_recv, x_send, x_recv, sib_send, sib_recv,
    halo_send, halo_recv, part_send, part_recv, l_send, l_recv, y_send, y_recv,
):
    ctx = lax.axis_index("ctx")
    fsdp = lax.axis_index("fsdp")
    y, l = lax.div(ctx, NL), lax.rem(ctx, NL)
    h, x, k = lax.div(fsdp, NX * 2), lax.rem(lax.div(fsdp, 2), NX), lax.rem(fsdp, 2)
    z = h * NL + l
    side = 1 - 2 * k

    def device(x_=None, y_=None, z_=None, k_=None):
        x_, y_ = (x if x_ is None else x_), (y if y_ is None else y_)
        z_, k_ = (z if z_ is None else z_), (k if k_ is None else k_)
        h_, l_ = lax.div(z_, NL), lax.rem(z_, NL)
        return (y_ * NL + l_, h_ * (NX * 2) + x_ * 2 + k_)

    def along(step):
        other = mod(ctx + step, NY * NL)
        return (other, fsdp)

    def remote(src, dst, send, recv, target):
        return pltpu.make_async_remote_copy(
            src_ref=src, dst_ref=dst, send_sem=send, recv_sem=recv, device_id=target, device_id_type=MESH
        )

    is_home = k == lax.rem(l, 2)

    barrier = pltpu.get_barrier_semaphore()

    def greet(target):
        pl.semaphore_signal(barrier, inc=1, device_id=target, device_id_type=MESH)

    near_x = (mod(x - 1, NX), mod(x + 1, NX))
    near_y = (mod(y - 1, NY), mod(y + 1, NY))
    for other in near_y:
        greet(device(y_=other))
    greet(device(x_=near_x[0]))
    for j in range(1, 5):
        greet(device(z_=mod(z - side * j, NZ), k_=lax.rem(l, 2)))
    greet(device(z_=mod(z - side * 4, NZ)))
    for other in near_x:
        greet(device(x_=other))
    greet(device(k_=1 - k))
    for i in range(1, NL):
        greet(device(z_=h * NL + mod(l + i, NL)))
    for i in range(1, NY):
        greet(device(y_=mod(y + i, NY)))
    greet(along(1))
    greet(along(-1))

    kvp = (keys[...].astype(F32) * values[...].astype(F32)).astype(BF16)
    kvx[ROWS:, :] = kvp
    rows_w[pl.ds(y, 1)] = weight[...].reshape(1, WIDE, WIDE)

    lane = lax.broadcasted_iota(jnp.int32, (TAPS, WIDE), 1)
    row = lax.broadcasted_iota(jnp.int32, (TAPS, WIDE), 0)
    plain = jnp.dot(filters[...], (lane == row).astype(BF16), preferred_element_type=F32)
    turned = jnp.dot(filters[...], (lane == TAPS - row).astype(BF16), preferred_element_type=F32)
    conv[0:GROUPS, :] = plain
    conv[GROUPS : 2 * GROUPS, :] = turned

    def build(g, _):
        line_b = jnp.broadcast_to(conv[pl.ds(g, 1), :], (ROWS, WIDE))
        line_z = jnp.broadcast_to(conv[pl.ds(GROUPS + g, 1), :], (ROWS, WIDE))
        toe_b[g] = pltpu.roll(line_b, 0, 1, stride=1, stride_axis=0).astype(BF16)
        toe_z[g] = pltpu.roll(line_z, 0, 1, stride=1, stride_axis=0).astype(BF16)
        return 0

    lax.fori_loop(0, GROUPS, build, 0)

    pl.semaphore_wait(barrier, 2 + 1 + 4 + 1 + 2 + 1 + (NL - 1) + (NY - 1) + 2)

    started = []

    def go_now(copy):
        copy.start()
        started.append(copy)

    def w_copy(direction, step, sub):
        owner = mod(y - step, NY) if direction == 0 else mod(y + step, NY)
        block = rows_w.at[owner, pl.ds(sub * ROWS, ROWS), :]
        return remote(
            block, block, w_send.at[direction, step, sub], w_recv.at[direction, step, sub],
            device(y_=near_y[1 - direction]),
        )

    def w_arrived(direction, step, sub):
        owner = mod(y - step, NY) if direction == 0 else mod(y + step, NY)
        block = rows_w.at[owner, pl.ds(sub * ROWS, ROWS), :]
        remote(
            block, block, w_send.at[direction, step - 1, sub], w_recv.at[direction, step - 1, sub],
            device(y_=near_y[1 - direction]),
        ).wait_recv()

    def piece(xs, k_, j, l_dest=None):
        l_dest = l if l_dest is None else l_dest
        z_from = mod(z - (1 - 2 * k_) * j, NZ)
        p = lax.rem(xs + 4 - lax.div(l_dest, 2), 2)
        x_from = mod(xs - p, NX)
        feature = 2 * lax.div(z_from, NL) + lax.div(x_from, 2)
        first = lax.rem(z_from, NL) * ROWS + p * HALF
        if j == 8:
            return grads.at[feature, pl.ds(pl.multiple_of(first + k_ * 32, 32), 32), :]
        return grads.at[feature, pl.ds(pl.multiple_of(first, HALF), HALF), :]

    def first_hop(p):
        src = go.at[pl.ds(0, HALF), :] if p == 0 else staged
        x_from = x if p == 0 else near_x[0]
        l_dest = 2 * lax.rem(x_from, 2) + k
        apart = mod(l_dest - l, NL)
        dst = grads.at[
            2 * h + lax.div(x_from, 2), pl.ds(pl.multiple_of(l * ROWS + p * HALF, HALF), HALF), :
        ]
        right = jnp.where(apart == 0, 4, apart)
        left = 4 - apart
        go_now(remote(src, dst, z1_send.at[p, 0], z_recv.at[right],
                      device(z_=mod(z + right, NZ), k_=0)))
        go_now(remote(src, dst, z1_send.at[p, 1], z_recv.at[left],
                      device(z_=mod(z - left, NZ), k_=1)))

    go_now(remote(go.at[pl.ds(HALF, HALF), :], staged, pre_send, pre_recv, device(x_=near_x[1])))
    first_hop(0)
    for sub in range(2):
        go_now(w_copy(0, 0, sub))
        go_now(w_copy(1, 0, 1 - sub))
    go_now(remote(kvx.at[pl.ds(ROWS, ROWS), :], kvx.at[pl.ds(0, ROWS), :],
                  halo_send.at[0], halo_recv.at[0], along(1)))
    remote(go.at[pl.ds(HALF, HALF), :], staged, pre_send, pre_recv, device(x_=near_x[1])).wait_recv()
    first_hop(1)

    def own_out(j):
        block = piece(x, k, j)
        return [
            remote(block, block, sib_send.at[0, j], sib_recv.at[0, j], device(k_=1 - k)),
            remote(block, block, x_send.at[0, j], x_recv.at[0, j], device(x_=near_x[1])),
            remote(block, block, x_send.at[1, j], x_recv.at[1, j], device(x_=near_x[0])),
        ]

    def own_event(j):
        block = piece(x, k, j)
        remote(block, block, z2_send.at[0], z_recv.at[j], device(k_=1 - k)).wait_recv()
        if j <= 4:
            farther = mod(z + side * 4, NZ)
            src = block
            if j == 4:
                z_from = mod(z - side * j, NZ)
                p = lax.rem(x + 4 - lax.div(l, 2), 2)
                feature = 2 * lax.div(z_from, NL) + lax.div(mod(x - p, NX), 2)
                first = lax.rem(z_from, NL) * ROWS + p * HALF + k * 32
                src = grads.at[feature, pl.ds(pl.multiple_of(first, 32), 32), :]
            go_now(remote(src, src, z2_send.at[j], z_recv.at[j + 4], device(z_=farther)))
        for copy in own_out(j):
            go_now(copy)

    def side_stream(index):
        return near_x[0] if index == 0 else near_x[1]

    first_x = jnp.where(k == 0, near_x[0], near_x[1])
    second_x = jnp.where(k == 0, near_x[1], near_x[0])
    onward = second_x
    across = mod(x + 2, NX)

    def first_out(j):
        block = piece(first_x, k, j)
        return [
            remote(block, block, x_send.at[2, j], x_recv.at[2, j], device(x_=onward)),
            remote(block, block, sib_send.at[1, j], sib_recv.at[1, j], device(k_=1 - k)),
        ]

    def second_out(j):
        block = piece(second_x, k, j)
        return [remote(block, block, sib_send.at[2, j], sib_recv.at[2, j], device(k_=1 - k))]

    def across_out(j):
        block = piece(across, k, j)
        return [remote(block, block, sib_send.at[3, j], sib_recv.at[3, j], device(k_=1 - k))]

    def arrived(block, slot, j):
        remote(block, block, x_send.at[0, j], x_recv.at[slot, j], device(k_=1 - k)).wait_recv()

    def side_event(j):
        arrived(piece(first_x, k, j), k, j)
        for copy in first_out(j):
            go_now(copy)
        arrived(piece(second_x, k, j), 1 - k, j)
        for copy in second_out(j):
            go_now(copy)

    def across_event(j):
        arrived(piece(across, k, j), 2, j)
        for copy in across_out(j):
            go_now(copy)

    def w_event(step, i):
        for direction in range(2):
            sub = i if direction == 0 else 1 - i
            w_arrived(direction, step, sub)
            if step < 3 or (step == 3 and i == 0):
                go_now(w_copy(direction, step, sub))

    @pl.when(is_home)
    def _():
        p = lax.rem(x + 4 - lax.div(l, 2), 2)
        block = piece(x, k, 0)
        block[...] = jnp.where(p == 0, go[0:HALF, :], staged[...])
        for copy in own_out(0):
            copy.start()

    def home_side():
        @pl.when(is_home)
        def _():
            arrived(piece(first_x, k, 0), k, 0)
            for copy in first_out(0):
                copy.start()
            arrived(piece(second_x, k, 0), 1 - k, 0)
            for copy in second_out(0):
                copy.start()

    def home_across():
        @pl.when(is_home)
        def _():
            arrived(piece(across, k, 0), 2, 0)
            for copy in across_out(0):
                copy.start()

    own_event(1)
    own_event(2)
    w_event(1, 0)
    own_event(3)
    home_side()
    w_event(1, 1)
    own_event(4)
    side_event(1)
    home_across()
    side_event(2)
    w_event(2, 0)
    own_event(5)
    side_event(3)
    across_event(1)
    w_event(2, 1)
    own_event(6)
    side_event(4)
    across_event(2)
    own_event(7)
    w_event(3, 0)
    side_event(5)
    across_event(3)
    own_event(8)
    w_event(3, 1)
    side_event(6)
    across_event(4)
    side_event(7)
    across_event(5)
    side_event(8)
    for j in (6, 7, 8):
        across_event(j)
    w_arrived(0, 4, 0)
    w_arrived(1, 4, 1)

    def from_sibling(stream, xs, j):
        block = piece(xs, 1 - k, j)
        remote(block, block, sib_send.at[stream, j], sib_recv.at[stream, j], device(k_=1 - k)).wait_recv()

    streams = ((0, x), (1, second_x), (2, first_x), (3, across))
    for j in range(1, 9):
        for stream, xs in streams:
            from_sibling(stream, xs, j)

    @pl.when(jnp.logical_not(is_home))
    def _():
        for stream, xs in streams:
            from_sibling(stream, xs, 0)

    def partial(tl):
        rows = pl.ds(pl.multiple_of(tl * ROWS, ROWS), ROWS)
        left = jnp.concatenate([grads[i, rows, :] for i in range(NY)], axis=1)
        right = rows_w[...].reshape(NY * WIDE, WIDE)
        return jnp.dot(left, right, preferred_element_type=F32)

    def part_copy(i):
        return remote(part.at[i - 1], part_in.at[i - 1], part_send.at[i - 1], part_recv.at[i - 1],
                      device(z_=h * NL + mod(l + i, NL)))

    for i in (2, 1, 3):
        part[i - 1] = partial(mod(l + i, NL)).astype(BF16)
        go_now(part_copy(i))
    mine = partial(l)

    remote(kvx.at[pl.ds(ROWS, ROWS), :], kvx.at[pl.ds(0, ROWS), :],
           halo_send.at[0], halo_recv.at[0], along(1)).wait_recv()
    kvx[0:ROWS, :] = jnp.where(ctx > 0, kvx[0:ROWS, :], jnp.zeros((ROWS, WIDE), BF16))
    group_of = lax.div(lax.broadcasted_iota(jnp.int32, (ROWS, WIDE), 1), WIDE // GROUPS)

    def forward(g, total):
        term = jnp.dot(toe_z[g], kvx[...], preferred_element_type=F32)
        return jnp.where(group_of == g, term, total)

    zeros = jnp.zeros((ROWS, WIDE), F32)
    conv[...] = lax.fori_loop(0, GROUPS, forward, zeros)
    flip = (
        lax.broadcasted_iota(jnp.int32, (WIDE, WIDE), 0) + lax.broadcasted_iota(jnp.int32, (WIDE, WIDE), 1)
        == WIDE - 1
    ).astype(BF16)
    kvrev[0:WIDE, :] = jnp.dot(flip, kvx[...], preferred_element_type=F32).astype(BF16)
    kvrev[WIDE:, :] = jnp.zeros((ROWS, WIDE), BF16)

    total = mine
    for i in (1, 2, 3):
        part_copy(i).wait_recv()
        total = total + part_in[i - 1].astype(F32)
    grad_y = total.astype(BF16).astype(F32)
    grad_z = (grad_y * queries[...].astype(F32)).astype(BF16)
    gzx[0:ROWS, :] = grad_z

    def later():
        return remote(gzx.at[pl.ds(0, ROWS), :], gzx.at[pl.ds(ROWS, ROWS), :],
                      halo_send.at[1], halo_recv.at[1], along(-1))

    go_now(later())
    out_q[...] = (grad_y * conv[...]).astype(BF16)

    keep = lax.div(lax.broadcasted_iota(jnp.int32, (WIDE, WIDE), 0), 16) == lax.div(
        lax.broadcasted_iota(jnp.int32, (WIDE, WIDE), 1), WIDE // GROUPS
    )
    cross = jnp.zeros((WIDE, WIDE), F32)
    for a in range(8):
        tokens = gzx[16 * a : 16 * a + 16, :]
        left = jnp.where(keep, jnp.concatenate([tokens] * GROUPS, axis=0), jnp.zeros((WIDE, WIDE), BF16))
        right = kvrev[112 - 16 * a : 112 - 16 * a + WIDE, :]
        cross = cross + lax.dot_general(left, right, (((1,), (1,)), ((), ())), preferred_element_type=F32)
    lines = []
    for g in range(GROUPS):
        turned_g = pltpu.roll(cross[16 * g : 16 * g + 16, :], WIDE - 15, 1, stride=1, stride_axis=0)
        lines.append(jnp.sum(turned_g, axis=0, keepdims=True)[:, 0:TAPS])
    sums_l[pl.ds(l, 1)] = jnp.concatenate(lines, axis=0).reshape(1, GROUPS, TAPS)

    def l_copy(i, slot):
        return remote(sums_l.at[slot], sums_l.at[slot], l_send.at[i - 1], l_recv.at[i - 1],
                      device(z_=h * NL + mod(l + i, NL)))

    def y_copy(i, slot):
        return remote(sums_y.at[slot], sums_y.at[slot], y_send.at[i - 1], y_recv.at[i - 1],
                      device(y_=mod(y + i, NY)))

    for i in range(1, NL):
        go_now(l_copy(i, l))

    def back_here(g, total_):
        term = jnp.dot(toe_b[g, :, 0:ROWS], gzx[0:ROWS, :], preferred_element_type=F32)
        return jnp.where(group_of == g, term, total_)

    conv[...] = lax.fori_loop(0, GROUPS, back_here, zeros)

    for i in range(1, NL):
        l_copy(i, mod(l - i, NL)).wait_recv()
    sums_y[pl.ds(y, 1)] = (((sums_l[0] + sums_l[1]) + sums_l[2]) + sums_l[3]).reshape(1, GROUPS, TAPS)
    for i in range(1, NY):
        go_now(y_copy(i, y))

    later().wait_recv()
    gzx[ROWS:, :] = jnp.where(ctx < NY * NL - 1, gzx[ROWS:, :], jnp.zeros((ROWS, WIDE), BF16))

    def back_later(g, total_):
        term = jnp.dot(toe_b[g, :, ROWS:], gzx[ROWS:, :], preferred_element_type=F32)
        return jnp.where(group_of == g, term, total_)

    grad_kv = conv[...] + lax.fori_loop(0, GROUPS, back_later, zeros)
    out_k[...] = (grad_kv * values[...].astype(F32)).astype(BF16)
    out_v[...] = (grad_kv * keys[...].astype(F32)).astype(BF16)

    for copy in started:
        copy.wait_send()

    @pl.when(is_home)
    def _():
        for copy in own_out(0) + first_out(0) + second_out(0) + across_out(0):
            copy.wait_send()

    for i in range(1, NY):
        y_copy(i, mod(y - i, NY)).wait_recv()
    final = sums_y[0]
    for i in range(1, NY):
        final = final + sums_y[i]
    out_f[...] = final


def per_device(*arrays):
    vmem = pl.BlockSpec(memory_space=pltpu.VMEM)
    dma = pltpu.SemaphoreType.DMA
    return pl.pallas_call(
        kernel,
        out_shape=(
            jax.ShapeDtypeStruct((ROWS, WIDE), BF16),
            jax.ShapeDtypeStruct((ROWS, WIDE), BF16),
            jax.ShapeDtypeStruct((ROWS, WIDE), BF16),
            jax.ShapeDtypeStruct((GROUPS, TAPS), F32),
        ),
        in_specs=[vmem] * 6,
        out_specs=(vmem,) * 4,
        scratch_shapes=[
            pltpu.VMEM((NY, NL * ROWS, WIDE), BF16),
            pltpu.VMEM((NY, WIDE, WIDE), BF16),
            pltpu.VMEM((HALF, WIDE), BF16),
            pltpu.VMEM((NL - 1, ROWS, WIDE), BF16),
            pltpu.VMEM((NL - 1, ROWS, WIDE), BF16),
            pltpu.VMEM((2 * ROWS, WIDE), BF16),
            pltpu.VMEM((3 * ROWS, WIDE), BF16),
            pltpu.VMEM((2 * ROWS, WIDE), BF16),
            pltpu.VMEM((GROUPS, ROWS, WIDE), BF16),
            pltpu.VMEM((GROUPS, ROWS, WIDE), BF16),
            pltpu.VMEM((ROWS, WIDE), F32),
            pltpu.VMEM((NL, GROUPS, TAPS), F32),
            pltpu.VMEM((NY, GROUPS, TAPS), F32),
            dma((2, 4, 2)), dma((2, 4, 2)), dma, dma, dma((2, 2)), dma((5,)), dma((9,)),
            dma((3, 9)), dma((3, 9)), dma((4, 9)), dma((4, 9)),
            dma((2,)), dma((2,)), dma((NL - 1,)), dma((NL - 1,)),
            dma((NL - 1,)), dma((NL - 1,)), dma((NY - 1,)), dma((NY - 1,)),
        ],
        compiler_params=pltpu.CompilerParams(collective_id=0, has_side_effects=True),
        name="block_backward",
    )(*arrays)


def solution(mesh):
    here = P("ctx", "fsdp")
    return jax.shard_map(
        per_device,
        mesh=mesh,
        in_specs=(here, here, here, here, P("fsdp", None), here),
        out_specs=(here, here, here, P("fsdp", None)),
        check_vma=False,
    )
```

```python
import jax
import jax.numpy as jnp
from jax import lax
from jax.experimental import pallas as pl
from jax.experimental.pallas import tpu as pltpu
from jax.sharding import PartitionSpec as P

MESH = pl.DeviceIdType.MESH
NX, NY, NH, NL = 4, 8, 4, 4
NZ = NH * NL
ROWS = 128
WIDE = 256
HALF = 64
GROUPS = 16
TAPS = 128
F32, BF16 = jnp.float32, jnp.bfloat16


def mod(value, size):
    return lax.rem(value + size, size)


def kernel(
    go_in, queries_in, keys_in, values_in, filters_in, weight_in,
    out_q, out_k, out_v, out_f,
    go, queries, keys, values, filters, load_sem, hello_y,
    grads, rows_w, part, part_in, kvx, kvrev, gzx, toe_z, toe_b, conv, sums_l, sums_y,
    w_send, w_recv, pre_send, pre_recv, z1_send, z2_send, z_recv, x_send, x_recv, sib_send, sib_recv,
    halo_send, halo_recv, part_send, part_recv, l_send, l_recv, y_send, y_recv,
):
    ctx = lax.axis_index("ctx")
    fsdp = lax.axis_index("fsdp")
    y, l = lax.div(ctx, NL), lax.rem(ctx, NL)
    h, x, k = lax.div(fsdp, NX * 2), lax.rem(lax.div(fsdp, 2), NX), lax.rem(fsdp, 2)
    z = h * NL + l
    side = 1 - 2 * k

    def device(x_=None, y_=None, z_=None, k_=None):
        x_, y_ = (x if x_ is None else x_), (y if y_ is None else y_)
        z_, k_ = (z if z_ is None else z_), (k if k_ is None else k_)
        h_, l_ = lax.div(z_, NL), lax.rem(z_, NL)
        return (y_ * NL + l_, h_ * (NX * 2) + x_ * 2 + k_)

    def along(step):
        other = mod(ctx + step, NY * NL)
        return (other, fsdp)

    def remote(src, dst, send, recv, target):
        return pltpu.make_async_remote_copy(
            src_ref=src, dst_ref=dst, send_sem=send, recv_sem=recv, device_id=target, device_id_type=MESH
        )

    is_home = k == lax.rem(l, 2)

    barrier = pltpu.get_barrier_semaphore()

    def greet(target):
        pl.semaphore_signal(barrier, inc=1, device_id=target, device_id_type=MESH)

    near_x = (mod(x - 1, NX), mod(x + 1, NX))
    near_y = (mod(y - 1, NY), mod(y + 1, NY))
    p_here = lax.rem(x + 4 - lax.div(l, 2), 2)
    for other in near_y:
        greet(device(y_=other))
    for other in near_x:
        greet(device(x_=other))
    greet(device(k_=1 - k))
    for j in range(1, 5):
        greet(device(x_=mod(x - p_here, NX), z_=mod(z - side * j, NZ), k_=lax.rem(l, 2)))
    greet(device(z_=mod(z - side * 4, NZ)))
    for i in range(1, NL):
        greet(device(z_=h * NL + mod(l + i, NL)))

    loads = [
        pltpu.make_async_copy(src, dst, load_sem.at[i])
        for i, (src, dst) in enumerate((
            (go_in, go), (weight_in, rows_w.at[y]), (keys_in, keys), (values_in, values),
            (filters_in, filters), (queries_in, queries),
        ))
    ]
    for load in loads:
        load.start()
    loads[0].wait()
    loads[1].wait()
    pl.semaphore_wait(barrier, 2 + 2 + 1 + 4 + 1 + (NL - 1))

    started = []

    def go_now(copy):
        copy.start()
        started.append(copy)

    def w_copy(direction, step, sub):
        owner = mod(y - step, NY) if direction == 0 else mod(y + step, NY)
        block = rows_w.at[owner, pl.ds(sub * ROWS, ROWS), :]
        return remote(
            block, block, w_send.at[direction, step, sub], w_recv.at[direction, step, sub],
            device(y_=near_y[1 - direction]),
        )

    def w_arrived(direction, step, sub):
        owner = mod(y - step, NY) if direction == 0 else mod(y + step, NY)
        block = rows_w.at[owner, pl.ds(sub * ROWS, ROWS), :]
        remote(
            block, block, w_send.at[direction, step - 1, sub], w_recv.at[direction, step - 1, sub],
            device(y_=near_y[1 - direction]),
        ).wait_recv()

    def piece(xs, k_, j, l_dest=None):
        l_dest = l if l_dest is None else l_dest
        z_from = mod(z - (1 - 2 * k_) * j, NZ)
        p = lax.rem(xs + 4 - lax.div(l_dest, 2), 2)
        x_from = mod(xs - p, NX)
        feature = 2 * lax.div(z_from, NL) + lax.div(x_from, 2)
        first = lax.rem(z_from, NL) * ROWS + p * HALF
        if j == 8:
            return grads.at[feature, pl.ds(pl.multiple_of(first + k_ * 32, 32), 32), :]
        return grads.at[feature, pl.ds(pl.multiple_of(first, HALF), HALF), :]

    def first_hop(p, direction):
        apart = mod(2 * lax.rem(x, 2) + k - l, NL)
        steps = jnp.where(apart == 0, 4, apart) if direction == 0 else 4 - apart
        target = mod(z + steps, NZ) if direction == 0 else mod(z - steps, NZ)
        dst = grads.at[
            2 * h + lax.div(x, 2), pl.ds(pl.multiple_of(l * ROWS + p * HALF, HALF), HALF), :
        ]
        return remote(go.at[pl.ds(p * HALF, HALF), :], dst, z1_send.at[p, direction], z_recv.at[steps],
                      device(x_=x if p == 0 else near_x[1], z_=target, k_=direction))

    home_half = 2 * lax.rem(x, 2) + k == l

    def pre_copy():
        dst = grads.at[
            2 * h + lax.div(x, 2), pl.ds(pl.multiple_of(l * ROWS + HALF, HALF), HALF), :
        ]
        return remote(go.at[pl.ds(HALF, HALF), :], dst, pre_send, pre_recv, device(x_=near_x[1]))

    @pl.when(home_half)
    def _():
        pre_copy().start()

    for p in range(2):
        for direction in range(2):
            go_now(first_hop(p, direction))
    for sub in range(2):
        go_now(w_copy(0, 0, sub))
        go_now(w_copy(1, 0, 1 - sub))

    @pl.when(l == NL - 1)
    def _():
        pl.semaphore_signal(hello_y, inc=1, device_id=device(y_=near_y[0]), device_id_type=MESH)

    for load in loads[2:]:
        load.wait()
    kvp = (keys[...].astype(F32) * values[...].astype(F32)).astype(BF16)
    kvx[ROWS:, :] = kvp

    lane = lax.broadcasted_iota(jnp.int32, (TAPS, WIDE), 1)
    row = lax.broadcasted_iota(jnp.int32, (TAPS, WIDE), 0)
    plain = jnp.dot(filters[...], (lane == row).astype(BF16), preferred_element_type=F32)
    turned = jnp.dot(filters[...], (lane == TAPS - row).astype(BF16), preferred_element_type=F32)
    conv[0:GROUPS, :] = plain
    conv[GROUPS : 2 * GROUPS, :] = turned

    def build(g, _):
        line_b = jnp.broadcast_to(conv[pl.ds(g, 1), :], (ROWS, WIDE))
        line_z = jnp.broadcast_to(conv[pl.ds(GROUPS + g, 1), :], (ROWS, WIDE))
        toe_b[g] = pltpu.roll(line_b, 0, 1, stride=1, stride_axis=0).astype(BF16)
        toe_z[g] = pltpu.roll(line_z, 0, 1, stride=1, stride_axis=0).astype(BF16)
        return 0

    lax.fori_loop(0, GROUPS, build, 0)


    def own_out(j):
        block = piece(x, k, j)
        return [
            remote(block, block, sib_send.at[0, j], sib_recv.at[0, j], device(k_=1 - k)),
            remote(block, block, x_send.at[0, j], x_recv.at[0, j], device(x_=near_x[1])),
            remote(block, block, x_send.at[1, j], x_recv.at[1, j], device(x_=near_x[0])),
        ]

    def own_event(j):
        block = piece(x, k, j)
        remote(block, block, z2_send.at[0], z_recv.at[j], device(k_=1 - k)).wait_recv()
        if j <= 4:
            farther = mod(z + side * 4, NZ)
            src = block
            if j == 4:
                z_from = mod(z - side * j, NZ)
                feature = 2 * lax.div(z_from, NL) + lax.div(mod(x - p_here, NX), 2)
                first = lax.rem(z_from, NL) * ROWS + p_here * HALF + k * 32
                src = grads.at[feature, pl.ds(pl.multiple_of(first, 32), 32), :]
            go_now(remote(src, src, z2_send.at[j], z_recv.at[j + 4], device(z_=farther)))
        for copy in own_out(j):
            go_now(copy)

    across = mod(x + 2, NX)

    def side_out(index, j):
        block = piece(near_x[index], k, j)
        copies = [remote(block, block, sib_send.at[1 + index, j], sib_recv.at[1 + index, j], device(k_=1 - k))]
        if j % 2 == index:
            copies.insert(0, remote(block, block, x_send.at[2, j], x_recv.at[2, j],
                                    device(x_=near_x[1 - index])))
        return copies

    def across_out(j):
        block = piece(across, k, j)
        return [remote(block, block, sib_send.at[3, j], sib_recv.at[3, j], device(k_=1 - k))]

    def arrived(block, slot, j):
        remote(block, block, x_send.at[0, j], x_recv.at[slot, j], device(k_=1 - k)).wait_recv()

    def side_event(j):
        for index in (j % 2, 1 - j % 2):
            arrived(piece(near_x[index], k, j), index, j)
            for copy in side_out(index, j):
                go_now(copy)

    def across_event(j):
        arrived(piece(across, k, j), 2, j)
        for copy in across_out(j):
            go_now(copy)

    def w_event(step, i):
        for direction in range(2):
            sub = i if direction == 0 else 1 - i
            w_arrived(direction, step, sub)
            if step < 3 or (step == 3 and i == 0):
                go_now(w_copy(direction, step, sub))

    @pl.when(is_home)
    def _():
        block = piece(x, k, 0)

        @pl.when(p_here == 0)
        def _():
            block[...] = go[0:HALF, :]

        @pl.when(p_here == 1)
        def _():
            remote(block, block, pre_send, pre_recv, device(x_=near_x[1])).wait_recv()

        for copy in own_out(0):
            copy.start()

    def home_side():
        @pl.when(is_home)
        def _():
            for index in range(2):
                arrived(piece(near_x[index], k, 0), index, 0)
                for copy in side_out(index, 0):
                    copy.start()

    def home_across():
        @pl.when(is_home)
        def _():
            arrived(piece(across, k, 0), 2, 0)
            for copy in across_out(0):
                copy.start()

    own_event(1)
    own_event(2)
    w_event(1, 0)
    own_event(3)
    home_side()
    w_event(1, 1)
    own_event(4)
    side_event(1)
    side_event(2)
    w_event(2, 0)
    side_event(3)
    home_across()

    kv_halo = remote(kvx.at[pl.ds(ROWS, ROWS), :], kvx.at[pl.ds(0, ROWS), :],
                     halo_send.at[0], halo_recv.at[0], along(1))

    @pl.when(l == NL - 1)
    def _():
        pl.semaphore_wait(hello_y, 1)

    go_now(kv_halo)

    side_event(4)
    w_event(2, 1)
    own_event(5)
    across_event(1)
    own_event(6)
    across_event(2)
    own_event(7)
    w_event(3, 0)
    across_event(3)
    own_event(8)
    w_event(3, 1)
    across_event(4)
    side_event(5)
    side_event(6)
    w_arrived(0, 4, 0)
    w_arrived(1, 4, 1)
    side_event(7)
    across_event(5)
    side_event(8)
    across_event(6)
    across_event(7)
    across_event(8)

    def from_sibling(stream, xs, j):
        block = piece(xs, 1 - k, j)
        remote(block, block, sib_send.at[stream, j], sib_recv.at[stream, j], device(k_=1 - k)).wait_recv()

    streams = ((0, x), (1, near_x[0]), (2, near_x[1]), (3, across))
    for j in range(1, 9):
        for stream, xs in streams:
            from_sibling(stream, xs, j)

    @pl.when(jnp.logical_not(is_home))
    def _():
        for stream, xs in streams:
            from_sibling(stream, xs, 0)

    def partial(tl):
        rows = pl.ds(pl.multiple_of(tl * ROWS, ROWS), ROWS)
        left = jnp.concatenate([grads[i, rows, :] for i in range(NY)], axis=1)
        right = rows_w[...].reshape(NY * WIDE, WIDE)
        return jnp.dot(left, right, preferred_element_type=F32)

    def part_copy(i):
        return remote(part.at[i - 1], part_in.at[i - 1], part_send.at[i - 1], part_recv.at[i - 1],
                      device(z_=h * NL + mod(l + i, NL)))

    for i in (2, 1, 3):
        part[i - 1] = partial(mod(l + i, NL)).astype(BF16)
        go_now(part_copy(i))
    mine = partial(l)

    kv_halo.wait_recv()
    kvx[0:ROWS, :] = jnp.where(ctx > 0, kvx[0:ROWS, :], jnp.zeros((ROWS, WIDE), BF16))
    group_of = lax.div(lax.broadcasted_iota(jnp.int32, (ROWS, WIDE), 1), WIDE // GROUPS)

    def forward(g, total):
        term = jnp.dot(toe_z[g], kvx[...], preferred_element_type=F32)
        return jnp.where(group_of == g, term, total)

    zeros = jnp.zeros((ROWS, WIDE), F32)
    conv[...] = lax.fori_loop(0, GROUPS, forward, zeros)
    flip = (
        lax.broadcasted_iota(jnp.int32, (WIDE, WIDE), 0) + lax.broadcasted_iota(jnp.int32, (WIDE, WIDE), 1)
        == WIDE - 1
    ).astype(BF16)
    kvrev[0:WIDE, :] = jnp.dot(flip, kvx[...], preferred_element_type=F32).astype(BF16)
    kvrev[WIDE:, :] = jnp.zeros((ROWS, WIDE), BF16)

    total = mine
    for i in (1, 2, 3):
        part_copy(i).wait_recv()
        total = total + part_in[i - 1].astype(F32)
    grad_y = total.astype(BF16).astype(F32)
    grad_z = (grad_y * queries[...].astype(F32)).astype(BF16)
    gzx[0:ROWS, :] = grad_z

    def later():
        return remote(gzx.at[pl.ds(0, ROWS), :], gzx.at[pl.ds(ROWS, ROWS), :],
                      halo_send.at[1], halo_recv.at[1], along(-1))

    go_now(later())
    out_q[...] = (grad_y * conv[...]).astype(BF16)

    keep = lax.div(lax.broadcasted_iota(jnp.int32, (WIDE, WIDE), 0), 16) == lax.div(
        lax.broadcasted_iota(jnp.int32, (WIDE, WIDE), 1), WIDE // GROUPS
    )
    cross = jnp.zeros((WIDE, WIDE), F32)
    for a in range(8):
        tokens = gzx[16 * a : 16 * a + 16, :]
        left = jnp.where(keep, jnp.concatenate([tokens] * GROUPS, axis=0), jnp.zeros((WIDE, WIDE), BF16))
        right = kvrev[112 - 16 * a : 112 - 16 * a + WIDE, :]
        cross = cross + lax.dot_general(left, right, (((1,), (1,)), ((), ())), preferred_element_type=F32)
    lines = []
    for g in range(GROUPS):
        turned_g = pltpu.roll(cross[16 * g : 16 * g + 16, :], WIDE - 15, 1, stride=1, stride_axis=0)
        lines.append(jnp.sum(turned_g, axis=0, keepdims=True)[:, 0:TAPS])
    sums_l[pl.ds(l, 1)] = jnp.concatenate(lines, axis=0).reshape(1, GROUPS, TAPS)

    def l_copy(i, slot):
        return remote(sums_l.at[slot], sums_l.at[slot], l_send.at[i - 1], l_recv.at[i - 1],
                      device(z_=h * NL + mod(l + i, NL)))

    def y_copy(i, slot):
        return remote(sums_y.at[slot], sums_y.at[slot], y_send.at[i - 1], y_recv.at[i - 1],
                      device(y_=mod(y + i, NY)))

    for i in range(1, NL):
        go_now(l_copy(i, l))

    def back_here(g, total_):
        term = jnp.dot(toe_b[g, :, 0:ROWS], gzx[0:ROWS, :], preferred_element_type=F32)
        return jnp.where(group_of == g, term, total_)

    conv[...] = lax.fori_loop(0, GROUPS, back_here, zeros)

    for i in range(1, NL):
        l_copy(i, mod(l - i, NL)).wait_recv()
    sums_y[pl.ds(y, 1)] = (((sums_l[0] + sums_l[1]) + sums_l[2]) + sums_l[3]).reshape(1, GROUPS, TAPS)
    for i in range(1, NY):
        go_now(y_copy(i, y))

    later().wait_recv()
    gzx[ROWS:, :] = jnp.where(ctx < NY * NL - 1, gzx[ROWS:, :], jnp.zeros((ROWS, WIDE), BF16))

    def back_later(g, total_):
        term = jnp.dot(toe_b[g, :, ROWS:], gzx[ROWS:, :], preferred_element_type=F32)
        return jnp.where(group_of == g, term, total_)

    grad_kv = conv[...] + lax.fori_loop(0, GROUPS, back_later, zeros)
    out_k[...] = (grad_kv * values[...].astype(F32)).astype(BF16)
    out_v[...] = (grad_kv * keys[...].astype(F32)).astype(BF16)

    for copy in started:
        copy.wait_send()

    @pl.when(is_home)
    def _():
        for copy in own_out(0) + side_out(0, 0) + side_out(1, 0) + across_out(0):
            copy.wait_send()

    @pl.when(home_half)
    def _():
        pre_copy().wait_send()

    for i in range(1, NY):
        y_copy(i, mod(y - i, NY)).wait_recv()
    final = sums_y[0]
    for i in range(1, NY):
        final = final + sums_y[i]
    out_f[...] = final


def hand_over(*refs):
    for src, dst in zip(refs[:4], refs[4:]):
        dst[...] = src[...]


def per_device(*arrays):
    vmem = pl.BlockSpec(memory_space=pltpu.VMEM)
    dma = pltpu.SemaphoreType.DMA
    results = pl.pallas_call(
        kernel,
        out_shape=(
            jax.ShapeDtypeStruct((ROWS, WIDE), BF16),
            jax.ShapeDtypeStruct((ROWS, WIDE), BF16),
            jax.ShapeDtypeStruct((ROWS, WIDE), BF16),
            jax.ShapeDtypeStruct((GROUPS, TAPS), F32),
        ),
        in_specs=[pl.BlockSpec(memory_space=pl.ANY)] * 6,
        out_specs=(vmem,) * 4,
        scratch_shapes=[
            pltpu.VMEM((ROWS, WIDE), BF16),
            pltpu.VMEM((ROWS, WIDE), BF16),
            pltpu.VMEM((ROWS, WIDE), BF16),
            pltpu.VMEM((ROWS, WIDE), BF16),
            pltpu.VMEM((GROUPS, TAPS), BF16),
            dma((6,)),
            pltpu.SemaphoreType.REGULAR,
            pltpu.VMEM((NY, NL * ROWS, WIDE), BF16),
            pltpu.VMEM((NY, WIDE, WIDE), BF16),
            pltpu.VMEM((NL - 1, ROWS, WIDE), BF16),
            pltpu.VMEM((NL - 1, ROWS, WIDE), BF16),
            pltpu.VMEM((2 * ROWS, WIDE), BF16),
            pltpu.VMEM((3 * ROWS, WIDE), BF16),
            pltpu.VMEM((2 * ROWS, WIDE), BF16),
            pltpu.VMEM((GROUPS, ROWS, WIDE), BF16),
            pltpu.VMEM((GROUPS, ROWS, WIDE), BF16),
            pltpu.VMEM((ROWS, WIDE), F32),
            pltpu.VMEM((NL, GROUPS, TAPS), F32),
            pltpu.VMEM((NY, GROUPS, TAPS), F32),
            dma((2, 4, 2)), dma((2, 4, 2)), dma, dma, dma((2, 2)), dma((5,)), dma((9,)),
            dma((3, 9)), dma((3, 9)), dma((4, 9)), dma((4, 9)),
            dma((2,)), dma((2,)), dma((NL - 1,)), dma((NL - 1,)),
            dma((NL - 1,)), dma((NL - 1,)), dma((NY - 1,)), dma((NY - 1,)),
        ],
        compiler_params=pltpu.CompilerParams(collective_id=0, has_side_effects=True),
        name="block_backward",
    )(*arrays)
    return pl.pallas_call(
        hand_over,
        out_shape=tuple(jax.ShapeDtypeStruct(a.shape, a.dtype) for a in results),
        in_specs=[vmem] * 4,
        out_specs=(vmem,) * 4,
        name="hand_over",
    )(*results)


def solution(mesh):
    here = P("ctx", "fsdp")
    return jax.shard_map(
        per_device,
        mesh=mesh,
        in_specs=(here, here, here, here, P("fsdp", None), here),
        out_specs=(here, here, here, P("fsdp", None)),
        check_vma=False,
    )
```

```python
import jax
import jax.numpy as jnp
from jax import lax
from jax.experimental import pallas as pl
from jax.experimental.pallas import tpu as pltpu
from jax.sharding import PartitionSpec as P

MESH = pl.DeviceIdType.MESH
NX, NY, NH, NL = 4, 8, 4, 4
NZ = NH * NL
ROWS = 128
WIDE = 256
HALF = 64
GROUPS = 16
TAPS = 128
F32, BF16 = jnp.float32, jnp.bfloat16


def mod(value, size):
    return lax.rem(value + size, size)


def kernel(
    go_in, queries_in, keys_in, values_in, filters_in, weight_in,
    out_q, out_k, out_v, out_f,
    go, queries, keys, values, filters, load_sem, hello_y,
    grads, rows_w, part, part_in, kvx, kvrev, gzx, toe_z, toe_b, conv, sums_l, sums_y,
    w_send, w_recv, pre_send, pre_recv, z1_send, z2_send, z_recv, x_send, x_recv, sib_send, sib_recv,
    halo_send, halo_recv, part_send, part_recv, l_send, l_recv, y_send, y_recv,
):
    ctx = lax.axis_index("ctx")
    fsdp = lax.axis_index("fsdp")
    y, l = lax.div(ctx, NL), lax.rem(ctx, NL)
    h, x, k = lax.div(fsdp, NX * 2), lax.rem(lax.div(fsdp, 2), NX), lax.rem(fsdp, 2)
    z = h * NL + l
    side = 1 - 2 * k

    def device(x_=None, y_=None, z_=None, k_=None):
        x_, y_ = (x if x_ is None else x_), (y if y_ is None else y_)
        z_, k_ = (z if z_ is None else z_), (k if k_ is None else k_)
        h_, l_ = lax.div(z_, NL), lax.rem(z_, NL)
        return (y_ * NL + l_, h_ * (NX * 2) + x_ * 2 + k_)

    def along(step):
        other = mod(ctx + step, NY * NL)
        return (other, fsdp)

    def remote(src, dst, send, recv, target):
        return pltpu.make_async_remote_copy(
            src_ref=src, dst_ref=dst, send_sem=send, recv_sem=recv, device_id=target, device_id_type=MESH
        )

    is_home = k == lax.rem(l, 2)

    barrier = pltpu.get_barrier_semaphore()

    def greet(target):
        pl.semaphore_signal(barrier, inc=1, device_id=target, device_id_type=MESH)

    near_x = (mod(x - 1, NX), mod(x + 1, NX))
    near_y = (mod(y - 1, NY), mod(y + 1, NY))
    p_here = lax.rem(x + 4 - lax.div(l, 2), 2)
    for other in near_y:
        greet(device(y_=other))
    for other in near_x:
        greet(device(x_=other))
    greet(device(k_=1 - k))
    for j in range(1, 5):
        greet(device(x_=mod(x - p_here, NX), z_=mod(z - side * j, NZ), k_=lax.rem(l, 2)))
    greet(device(z_=mod(z - side * 4, NZ)))
    for i in range(1, NL):
        greet(device(z_=h * NL + mod(l + i, NL)))

    loads = [
        pltpu.make_async_copy(src, dst, load_sem.at[i])
        for i, (src, dst) in enumerate((
            (go_in, go), (weight_in, rows_w.at[y]), (keys_in, keys), (values_in, values),
            (filters_in, filters), (queries_in, queries),
        ))
    ]
    for load in loads:
        load.start()
    loads[0].wait()
    loads[1].wait()
    pl.semaphore_wait(barrier, 2 + 2 + 1 + 4 + 1 + (NL - 1))

    started = []

    def go_now(copy):
        copy.start()
        started.append(copy)

    def w_copy(direction, step, sub):
        owner = mod(y - step, NY) if direction == 0 else mod(y + step, NY)
        block = rows_w.at[owner, pl.ds(sub * ROWS, ROWS), :]
        return remote(
            block, block, w_send.at[direction, step, sub], w_recv.at[direction, step, sub],
            device(y_=near_y[1 - direction]),
        )

    def w_arrived(direction, step, sub):
        owner = mod(y - step, NY) if direction == 0 else mod(y + step, NY)
        block = rows_w.at[owner, pl.ds(sub * ROWS, ROWS), :]
        remote(
            block, block, w_send.at[direction, step - 1, sub], w_recv.at[direction, step - 1, sub],
            device(y_=near_y[1 - direction]),
        ).wait_recv()

    def piece(xs, k_, j, l_dest=None):
        l_dest = l if l_dest is None else l_dest
        z_from = mod(z - (1 - 2 * k_) * j, NZ)
        p = lax.rem(xs + 4 - lax.div(l_dest, 2), 2)
        x_from = mod(xs - p, NX)
        feature = 2 * lax.div(z_from, NL) + lax.div(x_from, 2)
        first = lax.rem(z_from, NL) * ROWS + p * HALF
        if j == 8:
            return grads.at[feature, pl.ds(pl.multiple_of(first + k_ * 32, 32), 32), :]
        return grads.at[feature, pl.ds(pl.multiple_of(first, HALF), HALF), :]

    def first_hop(p, direction):
        apart = mod(2 * lax.rem(x, 2) + k - l, NL)
        steps = jnp.where(apart == 0, 4, apart) if direction == 0 else 4 - apart
        target = mod(z + steps, NZ) if direction == 0 else mod(z - steps, NZ)
        dst = grads.at[
            2 * h + lax.div(x, 2), pl.ds(pl.multiple_of(l * ROWS + p * HALF, HALF), HALF), :
        ]
        return remote(go.at[pl.ds(p * HALF, HALF), :], dst, z1_send.at[p, direction], z_recv.at[steps],
                      device(x_=x if p == 0 else near_x[1], z_=target, k_=direction))

    home_half = 2 * lax.rem(x, 2) + k == l

    def pre_copy():
        dst = grads.at[
            2 * h + lax.div(x, 2), pl.ds(pl.multiple_of(l * ROWS + HALF, HALF), HALF), :
        ]
        return remote(go.at[pl.ds(HALF, HALF), :], dst, pre_send, pre_recv, device(x_=near_x[1]))

    @pl.when(home_half)
    def _():
        pre_copy().start()

    for p in range(2):
        for direction in range(2):
            go_now(first_hop(p, direction))
    for sub in range(2):
        go_now(w_copy(0, 0, sub))
        go_now(w_copy(1, 0, 1 - sub))

    @pl.when(l == NL - 1)
    def _():
        pl.semaphore_signal(hello_y, inc=1, device_id=device(y_=near_y[0]), device_id_type=MESH)

    for load in loads[2:]:
        load.wait()
    kvp = (keys[...].astype(F32) * values[...].astype(F32)).astype(BF16)
    kvx[ROWS:, :] = kvp

    lane = lax.broadcasted_iota(jnp.int32, (TAPS, WIDE), 1)
    row = lax.broadcasted_iota(jnp.int32, (TAPS, WIDE), 0)
    plain = jnp.dot(filters[...], (lane == row).astype(BF16), preferred_element_type=F32)
    turned = jnp.dot(filters[...], (lane == TAPS - row).astype(BF16), preferred_element_type=F32)
    conv[0:GROUPS, :] = plain
    conv[GROUPS : 2 * GROUPS, :] = turned

    def build(g, _):
        line_b = jnp.broadcast_to(conv[pl.ds(g, 1), :], (ROWS, WIDE))
        line_z = jnp.broadcast_to(conv[pl.ds(GROUPS + g, 1), :], (ROWS, WIDE))
        toe_b[g] = pltpu.roll(line_b, 0, 1, stride=1, stride_axis=0).astype(BF16)
        toe_z[g] = pltpu.roll(line_z, 0, 1, stride=1, stride_axis=0).astype(BF16)
        return 0

    lax.fori_loop(0, GROUPS, build, 0)


    def own_out(j):
        block = piece(x, k, j)
        return [
            remote(block, block, x_send.at[0, j], x_recv.at[0, j], device(x_=near_x[1])),
            remote(block, block, x_send.at[1, j], x_recv.at[1, j], device(x_=near_x[0])),
            remote(block, block, sib_send.at[0, j], sib_recv.at[0, j], device(k_=1 - k)),
        ]

    def own_event(j):
        block = piece(x, k, j)
        remote(block, block, z2_send.at[0], z_recv.at[j], device(k_=1 - k)).wait_recv()
        if j <= 4:
            farther = mod(z + side * 4, NZ)
            src = block
            if j == 4:
                z_from = mod(z - side * j, NZ)
                feature = 2 * lax.div(z_from, NL) + lax.div(mod(x - p_here, NX), 2)
                first = lax.rem(z_from, NL) * ROWS + p_here * HALF + k * 32
                src = grads.at[feature, pl.ds(pl.multiple_of(first, 32), 32), :]
            go_now(remote(src, src, z2_send.at[j], z_recv.at[j + 4], device(z_=farther)))
        for copy in own_out(j):
            go_now(copy)

    across = mod(x + 2, NX)

    def side_out(index, j):
        block = piece(near_x[index], k, j)
        copies = [remote(block, block, sib_send.at[1 + index, j], sib_recv.at[1 + index, j], device(k_=1 - k))]
        if j % 2 == index:
            copies.insert(0, remote(block, block, x_send.at[2, j], x_recv.at[2, j],
                                    device(x_=near_x[1 - index])))
        return copies

    def across_out(j):
        block = piece(across, k, j)
        return [remote(block, block, sib_send.at[3, j], sib_recv.at[3, j], device(k_=1 - k))]

    def arrived(block, slot, j):
        remote(block, block, x_send.at[0, j], x_recv.at[slot, j], device(k_=1 - k)).wait_recv()

    def side_event(j):
        for index in (j % 2, 1 - j % 2):
            arrived(piece(near_x[index], k, j), index, j)
            for copy in side_out(index, j):
                go_now(copy)

    def across_event(j):
        arrived(piece(across, k, j), 2, j)
        for copy in across_out(j):
            go_now(copy)

    def w_event(step, i):
        for direction in range(2):
            sub = i if direction == 0 else 1 - i
            w_arrived(direction, step, sub)
            if step < 3 or (step == 3 and i == 0):
                go_now(w_copy(direction, step, sub))

    @pl.when(is_home)
    def _():
        block = piece(x, k, 0)

        @pl.when(p_here == 0)
        def _():
            block[...] = go[0:HALF, :]

        @pl.when(p_here == 1)
        def _():
            remote(block, block, pre_send, pre_recv, device(x_=near_x[1])).wait_recv()

        for copy in own_out(0):
            copy.start()

    def home_side():
        @pl.when(is_home)
        def _():
            for index in range(2):
                arrived(piece(near_x[index], k, 0), index, 0)
                for copy in side_out(index, 0):
                    copy.start()

    def home_across():
        @pl.when(is_home)
        def _():
            arrived(piece(across, k, 0), 2, 0)
            for copy in across_out(0):
                copy.start()

    own_event(1)
    own_event(2)
    own_event(3)
    own_event(4)
    w_event(1, 0)
    w_event(1, 1)
    home_side()
    side_event(1)
    side_event(2)
    own_event(5)
    side_event(3)
    own_event(6)
    side_event(4)
    own_event(7)
    home_across()

    kv_halo = remote(kvx.at[pl.ds(ROWS, ROWS), :], kvx.at[pl.ds(0, ROWS), :],
                     halo_send.at[0], halo_recv.at[0], along(1))

    @pl.when(l == NL - 1)
    def _():
        pl.semaphore_wait(hello_y, 1)

    go_now(kv_halo)

    own_event(8)
    w_event(2, 0)
    across_event(1)
    across_event(2)
    w_event(2, 1)
    across_event(3)
    across_event(4)
    side_event(5)
    side_event(6)
    side_event(7)
    side_event(8)
    w_event(3, 0)
    across_event(5)
    across_event(6)
    w_event(3, 1)
    across_event(7)
    across_event(8)
    w_arrived(0, 4, 0)
    w_arrived(1, 4, 1)

    def from_sibling(stream, xs, j):
        block = piece(xs, 1 - k, j)
        remote(block, block, sib_send.at[stream, j], sib_recv.at[stream, j], device(k_=1 - k)).wait_recv()

    streams = ((0, x), (1, near_x[0]), (2, near_x[1]), (3, across))
    for j in range(1, 9):
        for stream, xs in streams:
            from_sibling(stream, xs, j)

    @pl.when(jnp.logical_not(is_home))
    def _():
        for stream, xs in streams:
            from_sibling(stream, xs, 0)

    def partial(tl):
        rows = pl.ds(pl.multiple_of(tl * ROWS, ROWS), ROWS)
        left = jnp.concatenate([grads[i, rows, :] for i in range(NY)], axis=1)
        right = rows_w[...].reshape(NY * WIDE, WIDE)
        return jnp.dot(left, right, preferred_element_type=F32)

    def part_copy(i):
        return remote(part.at[i - 1], part_in.at[i - 1], part_send.at[i - 1], part_recv.at[i - 1],
                      device(z_=h * NL + mod(l + i, NL)))

    for i in (2, 1, 3):
        part[i - 1] = partial(mod(l + i, NL)).astype(BF16)
        go_now(part_copy(i))
    mine = partial(l)

    kv_halo.wait_recv()
    kvx[0:ROWS, :] = jnp.where(ctx > 0, kvx[0:ROWS, :], jnp.zeros((ROWS, WIDE), BF16))
    group_of = lax.div(lax.broadcasted_iota(jnp.int32, (ROWS, WIDE), 1), WIDE // GROUPS)

    def forward(g, total):
        term = jnp.dot(toe_z[g], kvx[...], preferred_element_type=F32)
        return jnp.where(group_of == g, term, total)

    zeros = jnp.zeros((ROWS, WIDE), F32)
    conv[...] = lax.fori_loop(0, GROUPS, forward, zeros)
    flip = (
        lax.broadcasted_iota(jnp.int32, (WIDE, WIDE), 0) + lax.broadcasted_iota(jnp.int32, (WIDE, WIDE), 1)
        == WIDE - 1
    ).astype(BF16)
    kvrev[0:WIDE, :] = jnp.dot(flip, kvx[...], preferred_element_type=F32).astype(BF16)
    kvrev[WIDE:, :] = jnp.zeros((ROWS, WIDE), BF16)

    total = mine
    for i in (1, 2, 3):
        part_copy(i).wait_recv()
        total = total + part_in[i - 1].astype(F32)
    grad_y = total.astype(BF16).astype(F32)
    grad_z = (grad_y * queries[...].astype(F32)).astype(BF16)
    gzx[0:ROWS, :] = grad_z

    def later():
        return remote(gzx.at[pl.ds(0, ROWS), :], gzx.at[pl.ds(ROWS, ROWS), :],
                      halo_send.at[1], halo_recv.at[1], along(-1))

    go_now(later())
    out_q[...] = (grad_y * conv[...]).astype(BF16)

    keep = lax.div(lax.broadcasted_iota(jnp.int32, (WIDE, WIDE), 0), 16) == lax.div(
        lax.broadcasted_iota(jnp.int32, (WIDE, WIDE), 1), WIDE // GROUPS
    )
    cross = jnp.zeros((WIDE, WIDE), F32)
    for a in range(8):
        tokens = gzx[16 * a : 16 * a + 16, :]
        left = jnp.where(keep, jnp.concatenate([tokens] * GROUPS, axis=0), jnp.zeros((WIDE, WIDE), BF16))
        right = kvrev[112 - 16 * a : 112 - 16 * a + WIDE, :]
        cross = cross + lax.dot_general(left, right, (((1,), (1,)), ((), ())), preferred_element_type=F32)
    lines = []
    for g in range(GROUPS):
        turned_g = pltpu.roll(cross[16 * g : 16 * g + 16, :], WIDE - 15, 1, stride=1, stride_axis=0)
        lines.append(jnp.sum(turned_g, axis=0, keepdims=True)[:, 0:TAPS])
    sums_l[pl.ds(l, 1)] = jnp.concatenate(lines, axis=0).reshape(1, GROUPS, TAPS)

    def l_copy(i, slot):
        return remote(sums_l.at[slot], sums_l.at[slot], l_send.at[i - 1], l_recv.at[i - 1],
                      device(z_=h * NL + mod(l + i, NL)))

    def y_copy(i, slot):
        return remote(sums_y.at[slot], sums_y.at[slot], y_send.at[i - 1], y_recv.at[i - 1],
                      device(y_=mod(y + i, NY)))

    for i in range(1, NL):
        go_now(l_copy(i, l))

    def back_here(g, total_):
        term = jnp.dot(toe_b[g, :, 0:ROWS], gzx[0:ROWS, :], preferred_element_type=F32)
        return jnp.where(group_of == g, term, total_)

    conv[...] = lax.fori_loop(0, GROUPS, back_here, zeros)

    for i in range(1, NL):
        l_copy(i, mod(l - i, NL)).wait_recv()
    sums_y[pl.ds(y, 1)] = (((sums_l[0] + sums_l[1]) + sums_l[2]) + sums_l[3]).reshape(1, GROUPS, TAPS)
    for i in range(1, NY):
        go_now(y_copy(i, y))

    later().wait_recv()
    gzx[ROWS:, :] = jnp.where(ctx < NY * NL - 1, gzx[ROWS:, :], jnp.zeros((ROWS, WIDE), BF16))

    def back_later(g, total_):
        term = jnp.dot(toe_b[g, :, ROWS:], gzx[ROWS:, :], preferred_element_type=F32)
        return jnp.where(group_of == g, term, total_)

    grad_kv = conv[...] + lax.fori_loop(0, GROUPS, back_later, zeros)
    out_k[...] = (grad_kv * values[...].astype(F32)).astype(BF16)
    out_v[...] = (grad_kv * keys[...].astype(F32)).astype(BF16)

    for copy in started:
        copy.wait_send()

    @pl.when(is_home)
    def _():
        for copy in own_out(0) + side_out(0, 0) + side_out(1, 0) + across_out(0):
            copy.wait_send()

    @pl.when(home_half)
    def _():
        pre_copy().wait_send()

    for i in range(1, NY):
        y_copy(i, mod(y - i, NY)).wait_recv()
    final = sums_y[0]
    for i in range(1, NY):
        final = final + sums_y[i]
    out_f[...] = final


def hand_over(*refs):
    for src, dst in zip(refs[:4], refs[4:]):
        dst[...] = src[...]


def per_device(*arrays):
    vmem = pl.BlockSpec(memory_space=pltpu.VMEM)
    dma = pltpu.SemaphoreType.DMA
    results = pl.pallas_call(
        kernel,
        out_shape=(
            jax.ShapeDtypeStruct((ROWS, WIDE), BF16),
            jax.ShapeDtypeStruct((ROWS, WIDE), BF16),
            jax.ShapeDtypeStruct((ROWS, WIDE), BF16),
            jax.ShapeDtypeStruct((GROUPS, TAPS), F32),
        ),
        in_specs=[pl.BlockSpec(memory_space=pl.ANY)] * 6,
        out_specs=(vmem,) * 4,
        scratch_shapes=[
            pltpu.VMEM((ROWS, WIDE), BF16),
            pltpu.VMEM((ROWS, WIDE), BF16),
            pltpu.VMEM((ROWS, WIDE), BF16),
            pltpu.VMEM((ROWS, WIDE), BF16),
            pltpu.VMEM((GROUPS, TAPS), BF16),
            dma((6,)),
            pltpu.SemaphoreType.REGULAR,
            pltpu.VMEM((NY, NL * ROWS, WIDE), BF16),
            pltpu.VMEM((NY, WIDE, WIDE), BF16),
            pltpu.VMEM((NL - 1, ROWS, WIDE), BF16),
            pltpu.VMEM((NL - 1, ROWS, WIDE), BF16),
            pltpu.VMEM((2 * ROWS, WIDE), BF16),
            pltpu.VMEM((3 * ROWS, WIDE), BF16),
            pltpu.VMEM((2 * ROWS, WIDE), BF16),
            pltpu.VMEM((GROUPS, ROWS, WIDE), BF16),
            pltpu.VMEM((GROUPS, ROWS, WIDE), BF16),
            pltpu.VMEM((ROWS, WIDE), F32),
            pltpu.VMEM((NL, GROUPS, TAPS), F32),
            pltpu.VMEM((NY, GROUPS, TAPS), F32),
            dma((2, 4, 2)), dma((2, 4, 2)), dma, dma, dma((2, 2)), dma((5,)), dma((9,)),
            dma((3, 9)), dma((3, 9)), dma((4, 9)), dma((4, 9)),
            dma((2,)), dma((2,)), dma((NL - 1,)), dma((NL - 1,)),
            dma((NL - 1,)), dma((NL - 1,)), dma((NY - 1,)), dma((NY - 1,)),
        ],
        compiler_params=pltpu.CompilerParams(collective_id=0, has_side_effects=True),
        name="block_backward",
    )(*arrays)
    return pl.pallas_call(
        hand_over,
        out_shape=tuple(jax.ShapeDtypeStruct(a.shape, a.dtype) for a in results),
        in_specs=[vmem] * 4,
        out_specs=(vmem,) * 4,
        name="hand_over",
    )(*results)


def solution(mesh):
    here = P("ctx", "fsdp")
    return jax.shard_map(
        per_device,
        mesh=mesh,
        in_specs=(here, here, here, here, P("fsdp", None), here),
        out_specs=(here, here, here, P("fsdp", None)),
        check_vma=False,
    )
```

```python
import jax
import jax.numpy as jnp
from jax import lax
from jax.experimental import pallas as pl
from jax.experimental.pallas import tpu as pltpu
from jax.sharding import PartitionSpec as P

MESH = pl.DeviceIdType.MESH
NX, NY, NH, NL = 4, 8, 4, 4
NZ = NH * NL
ROWS = 128
WIDE = 256
HALF = 64
GROUPS = 16
TAPS = 128
F32, BF16 = jnp.float32, jnp.bfloat16


def mod(value, size):
    return lax.rem(value + size, size)


def kernel(
    go_in, queries_in, keys_in, values_in, filters_in, weight_in,
    out_q, out_k, out_v, out_f,
    go, queries, keys, values, filters, load_sem, hello_y,
    grads, rows_w, part, part_in, kvx, kvrev, gzx, toe_z, toe_b, conv, sums_l, sums_y,
    w_send, w_recv, pre_send, pre_recv, z1_send, z2_send, z_recv, x_send, x_recv, sib_send, sib_recv,
    halo_send, halo_recv, part_send, part_recv, l_send, l_recv, y_send, y_recv,
):
    ctx = lax.axis_index("ctx")
    fsdp = lax.axis_index("fsdp")
    y, l = lax.div(ctx, NL), lax.rem(ctx, NL)
    h, x, k = lax.div(fsdp, NX * 2), lax.rem(lax.div(fsdp, 2), NX), lax.rem(fsdp, 2)
    z = h * NL + l
    side = 1 - 2 * k

    def device(x_=None, y_=None, z_=None, k_=None):
        x_, y_ = (x if x_ is None else x_), (y if y_ is None else y_)
        z_, k_ = (z if z_ is None else z_), (k if k_ is None else k_)
        h_, l_ = lax.div(z_, NL), lax.rem(z_, NL)
        return (y_ * NL + l_, h_ * (NX * 2) + x_ * 2 + k_)

    def along(step):
        other = mod(ctx + step, NY * NL)
        return (other, fsdp)

    def remote(src, dst, send, recv, target):
        return pltpu.make_async_remote_copy(
            src_ref=src, dst_ref=dst, send_sem=send, recv_sem=recv, device_id=target, device_id_type=MESH
        )

    is_home = k == lax.rem(l, 2)

    barrier = pltpu.get_barrier_semaphore()

    def greet(target):
        pl.semaphore_signal(barrier, inc=1, device_id=target, device_id_type=MESH)

    near_x = (mod(x - 1, NX), mod(x + 1, NX))
    near_y = (mod(y - 1, NY), mod(y + 1, NY))
    p_here = lax.rem(x + 4 - lax.div(l, 2), 2)
    for other in near_y:
        greet(device(y_=other))
    for other in near_x:
        greet(device(x_=other))
    greet(device(k_=1 - k))
    for j in range(1, 5):
        greet(device(x_=mod(x - p_here, NX), z_=mod(z - side * j, NZ), k_=lax.rem(l, 2)))
    greet(device(z_=mod(z - side * 4, NZ)))
    for i in range(1, NL):
        greet(device(z_=h * NL + mod(l + i, NL)))

    loads = [
        pltpu.make_async_copy(src, dst, load_sem.at[i])
        for i, (src, dst) in enumerate((
            (go_in, go), (weight_in, rows_w.at[y]), (keys_in, keys), (values_in, values),
            (filters_in, filters), (queries_in, queries),
        ))
    ]
    for load in loads:
        load.start()
    loads[0].wait()
    loads[1].wait()
    pl.semaphore_wait(barrier, 2 + 2 + 1 + 4 + 1 + (NL - 1))

    started = []

    def go_now(copy):
        copy.start()
        started.append(copy)

    def w_copy(direction, step, sub):
        owner = mod(y - step, NY) if direction == 0 else mod(y + step, NY)
        block = rows_w.at[owner, pl.ds(sub * ROWS, ROWS), :]
        return remote(
            block, block, w_send.at[direction, step, sub], w_recv.at[direction, step, sub],
            device(y_=near_y[1 - direction]),
        )

    def w_arrived(direction, step, sub):
        owner = mod(y - step, NY) if direction == 0 else mod(y + step, NY)
        block = rows_w.at[owner, pl.ds(sub * ROWS, ROWS), :]
        remote(
            block, block, w_send.at[direction, step - 1, sub], w_recv.at[direction, step - 1, sub],
            device(y_=near_y[1 - direction]),
        ).wait_recv()

    def piece(xs, k_, j, l_dest=None):
        l_dest = l if l_dest is None else l_dest
        z_from = mod(z - (1 - 2 * k_) * j, NZ)
        p = lax.rem(xs + 4 - lax.div(l_dest, 2), 2)
        x_from = mod(xs - p, NX)
        feature = 2 * lax.div(z_from, NL) + lax.div(x_from, 2)
        first = lax.rem(z_from, NL) * ROWS + p * HALF
        if j == 8:
            return grads.at[feature, pl.ds(pl.multiple_of(first + k_ * 32, 32), 32), :]
        return grads.at[feature, pl.ds(pl.multiple_of(first, HALF), HALF), :]

    def first_hop(p, direction):
        apart = mod(2 * lax.rem(x, 2) + k - l, NL)
        steps = jnp.where(apart == 0, 4, apart) if direction == 0 else 4 - apart
        target = mod(z + steps, NZ) if direction == 0 else mod(z - steps, NZ)
        dst = grads.at[
            2 * h + lax.div(x, 2), pl.ds(pl.multiple_of(l * ROWS + p * HALF, HALF), HALF), :
        ]
        return remote(go.at[pl.ds(p * HALF, HALF), :], dst, z1_send.at[p, direction], z_recv.at[steps],
                      device(x_=x if p == 0 else near_x[1], z_=target, k_=direction))

    home_half = 2 * lax.rem(x, 2) + k == l

    def pre_copy():
        dst = grads.at[
            2 * h + lax.div(x, 2), pl.ds(pl.multiple_of(l * ROWS + HALF, HALF), HALF), :
        ]
        return remote(go.at[pl.ds(HALF, HALF), :], dst, pre_send, pre_recv, device(x_=near_x[1]))

    @pl.when(home_half)
    def _():
        pre_copy().start()

    for p in range(2):
        for direction in range(2):
            go_now(first_hop(p, direction))
    for sub in range(2):
        go_now(w_copy(0, 0, sub))
        go_now(w_copy(1, 0, 1 - sub))

    @pl.when(l == NL - 1)
    def _():
        pl.semaphore_signal(hello_y, inc=1, device_id=device(y_=near_y[0]), device_id_type=MESH)

    for load in loads[2:]:
        load.wait()
    kvp = (keys[...].astype(F32) * values[...].astype(F32)).astype(BF16)
    kvx[ROWS:, :] = kvp

    lane = lax.broadcasted_iota(jnp.int32, (TAPS, WIDE), 1)
    row = lax.broadcasted_iota(jnp.int32, (TAPS, WIDE), 0)
    plain = jnp.dot(filters[...], (lane == row).astype(BF16), preferred_element_type=F32)
    turned = jnp.dot(filters[...], (lane == TAPS - row).astype(BF16), preferred_element_type=F32)
    conv[0:GROUPS, :] = plain
    conv[GROUPS : 2 * GROUPS, :] = turned

    def build(g, _):
        line_b = jnp.broadcast_to(conv[pl.ds(g, 1), :], (ROWS, WIDE))
        line_z = jnp.broadcast_to(conv[pl.ds(GROUPS + g, 1), :], (ROWS, WIDE))
        toe_b[g] = pltpu.roll(line_b, 0, 1, stride=1, stride_axis=0).astype(BF16)
        toe_z[g] = pltpu.roll(line_z, 0, 1, stride=1, stride_axis=0).astype(BF16)
        return 0

    lax.fori_loop(0, GROUPS, build, 0)


    def own_out(j):
        block = piece(x, k, j)
        return [
            remote(block, block, x_send.at[0, j], x_recv.at[0, j], device(x_=near_x[1])),
            remote(block, block, x_send.at[1, j], x_recv.at[1, j], device(x_=near_x[0])),
            remote(block, block, sib_send.at[0, j], sib_recv.at[0, j], device(k_=1 - k)),
        ]

    def own_event(j):
        block = piece(x, k, j)
        remote(block, block, z2_send.at[0], z_recv.at[j], device(k_=1 - k)).wait_recv()
        if j <= 4:
            farther = mod(z + side * 4, NZ)
            src = block
            if j == 4:
                z_from = mod(z - side * j, NZ)
                feature = 2 * lax.div(z_from, NL) + lax.div(mod(x - p_here, NX), 2)
                first = lax.rem(z_from, NL) * ROWS + p_here * HALF + k * 32
                src = grads.at[feature, pl.ds(pl.multiple_of(first, 32), 32), :]
            go_now(remote(src, src, z2_send.at[j], z_recv.at[j + 4], device(z_=farther)))
        for copy in own_out(j):
            go_now(copy)

    across = mod(x + 2, NX)

    def side_out(index, j):
        block = piece(near_x[index], k, j)
        copies = [remote(block, block, sib_send.at[1 + index, j], sib_recv.at[1 + index, j], device(k_=1 - k))]
        if j % 2 == index:
            copies.insert(0, remote(block, block, x_send.at[2, j], x_recv.at[2, j],
                                    device(x_=near_x[1 - index])))
        return copies

    def across_out(j):
        block = piece(across, k, j)
        return [remote(block, block, sib_send.at[3, j], sib_recv.at[3, j], device(k_=1 - k))]

    def arrived(block, slot, j):
        remote(block, block, x_send.at[0, j], x_recv.at[slot, j], device(k_=1 - k)).wait_recv()

    def side_event(j):
        for index in (j % 2, 1 - j % 2):
            arrived(piece(near_x[index], k, j), index, j)
            for copy in side_out(index, j):
                go_now(copy)

    def across_event(j):
        arrived(piece(across, k, j), 2, j)
        for copy in across_out(j):
            go_now(copy)

    def w_event(step, i):
        for direction in range(2):
            sub = i if direction == 0 else 1 - i
            w_arrived(direction, step, sub)
            if step < 3 or (step == 3 and i == 0):
                go_now(w_copy(direction, step, sub))

    @pl.when(is_home)
    def _():
        block = piece(x, k, 0)

        @pl.when(p_here == 0)
        def _():
            block[...] = go[0:HALF, :]

        @pl.when(p_here == 1)
        def _():
            remote(block, block, pre_send, pre_recv, device(x_=near_x[1])).wait_recv()

        for copy in own_out(0):
            copy.start()

    def home_side():
        @pl.when(is_home)
        def _():
            for index in range(2):
                arrived(piece(near_x[index], k, 0), index, 0)
                for copy in side_out(index, 0):
                    copy.start()

    def home_across():
        @pl.when(is_home)
        def _():
            arrived(piece(across, k, 0), 2, 0)
            for copy in across_out(0):
                copy.start()

    own_event(1)
    own_event(2)
    own_event(3)
    own_event(4)
    w_event(1, 0)
    w_event(1, 1)
    home_side()
    side_event(1)
    side_event(2)
    own_event(5)
    side_event(3)
    own_event(6)
    side_event(4)
    own_event(7)
    home_across()

    kv_halo = remote(kvx.at[pl.ds(ROWS, ROWS), :], kvx.at[pl.ds(0, ROWS), :],
                     halo_send.at[0], halo_recv.at[0], along(1))

    @pl.when(l == NL - 1)
    def _():
        pl.semaphore_wait(hello_y, 1)

    go_now(kv_halo)

    own_event(8)
    w_event(2, 0)
    across_event(1)
    across_event(2)
    w_event(2, 1)
    across_event(3)
    across_event(4)
    side_event(5)
    side_event(6)
    side_event(7)
    side_event(8)
    w_event(3, 0)
    across_event(5)
    across_event(6)
    w_event(3, 1)
    across_event(7)
    across_event(8)
    w_arrived(0, 4, 0)
    w_arrived(1, 4, 1)

    def from_sibling(stream, xs, j):
        block = piece(xs, 1 - k, j)
        remote(block, block, sib_send.at[stream, j], sib_recv.at[stream, j], device(k_=1 - k)).wait_recv()

    streams = ((0, x), (1, near_x[0]), (2, near_x[1]), (3, across))
    for j in range(1, 9):
        for stream, xs in streams:
            from_sibling(stream, xs, j)

    @pl.when(jnp.logical_not(is_home))
    def _():
        for stream, xs in streams:
            from_sibling(stream, xs, 0)

    def partial(tl):
        rows = pl.ds(pl.multiple_of(tl * ROWS, ROWS), ROWS)
        left = jnp.concatenate([grads[i, rows, :] for i in range(NY)], axis=1)
        right = rows_w[...].reshape(NY * WIDE, WIDE)
        return jnp.dot(left, right, preferred_element_type=F32)

    def part_copy(i):
        return remote(part.at[i - 1], part_in.at[i - 1], part_send.at[i - 1], part_recv.at[i - 1],
                      device(z_=h * NL + mod(l + i, NL)))

    for i in (2, 1, 3):
        part[i - 1] = partial(mod(l + i, NL)).astype(BF16)
        go_now(part_copy(i))
    mine = partial(l)

    kv_halo.wait_recv()
    kvx[0:ROWS, :] = jnp.where(ctx > 0, kvx[0:ROWS, :], jnp.zeros((ROWS, WIDE), BF16))
    group_of = lax.div(lax.broadcasted_iota(jnp.int32, (ROWS, WIDE), 1), WIDE // GROUPS)

    def forward(g, total):
        term = jnp.dot(toe_z[g], kvx[...], preferred_element_type=F32)
        return jnp.where(group_of == g, term, total)

    zeros = jnp.zeros((ROWS, WIDE), F32)
    conv[...] = lax.fori_loop(0, GROUPS, forward, zeros)
    flip = (
        lax.broadcasted_iota(jnp.int32, (WIDE, WIDE), 0) + lax.broadcasted_iota(jnp.int32, (WIDE, WIDE), 1)
        == WIDE - 1
    ).astype(BF16)
    kvrev[0:WIDE, :] = jnp.dot(flip, kvx[...], preferred_element_type=F32).astype(BF16)
    kvrev[WIDE:, :] = jnp.zeros((ROWS, WIDE), BF16)

    total = mine
    for i in (1, 2, 3):
        part_copy(i).wait_recv()
        total = total + part_in[i - 1].astype(F32)
    grad_y = total.astype(BF16).astype(F32)
    grad_z = (grad_y * queries[...].astype(F32)).astype(BF16)
    gzx[0:ROWS, :] = grad_z

    def later():
        return remote(gzx.at[pl.ds(0, ROWS), :], gzx.at[pl.ds(ROWS, ROWS), :],
                      halo_send.at[1], halo_recv.at[1], along(-1))

    go_now(later())
    out_q[...] = (grad_y * conv[...]).astype(BF16)

    keep = lax.div(lax.broadcasted_iota(jnp.int32, (WIDE, WIDE), 0), 16) == lax.div(
        lax.broadcasted_iota(jnp.int32, (WIDE, WIDE), 1), WIDE // GROUPS
    )
    cross = jnp.zeros((WIDE, WIDE), F32)
    for a in range(8):
        tokens = gzx[16 * a : 16 * a + 16, :]
        left = jnp.where(keep, jnp.concatenate([tokens] * GROUPS, axis=0), jnp.zeros((WIDE, WIDE), BF16))
        right = kvrev[112 - 16 * a : 112 - 16 * a + WIDE, :]
        cross = cross + lax.dot_general(left, right, (((1,), (1,)), ((), ())), preferred_element_type=F32)
    lines = []
    for g in range(GROUPS):
        turned_g = pltpu.roll(cross[16 * g : 16 * g + 16, :], WIDE - 15, 1, stride=1, stride_axis=0)
        lines.append(jnp.sum(turned_g, axis=0, keepdims=True)[:, 0:TAPS])
    sums_l[pl.ds(l, 1)] = jnp.concatenate(lines, axis=0).reshape(1, GROUPS, TAPS)

    def l_copy(i, slot):
        return remote(sums_l.at[slot], sums_l.at[slot], l_send.at[i - 1], l_recv.at[i - 1],
                      device(z_=h * NL + mod(l + i, NL)))

    def y_copy(i, slot):
        return remote(sums_y.at[slot], sums_y.at[slot], y_send.at[i - 1], y_recv.at[i - 1],
                      device(y_=mod(y + i, NY)))

    for i in range(1, NL):
        go_now(l_copy(i, l))

    def back_here(g, total_):
        term = jnp.dot(toe_b[g, :, 0:ROWS], gzx[0:ROWS, :], preferred_element_type=F32)
        return jnp.where(group_of == g, term, total_)

    conv[...] = lax.fori_loop(0, GROUPS, back_here, zeros)

    for i in range(1, NL):
        l_copy(i, mod(l - i, NL)).wait_recv()
    sums_y[pl.ds(y, 1)] = (((sums_l[0] + sums_l[1]) + sums_l[2]) + sums_l[3]).reshape(1, GROUPS, TAPS)
    for i in range(1, NY):
        go_now(y_copy(i, y))

    later().wait_recv()
    gzx[ROWS:, :] = jnp.where(ctx < NY * NL - 1, gzx[ROWS:, :], jnp.zeros((ROWS, WIDE), BF16))

    def back_later(g, total_):
        term = jnp.dot(toe_b[g, :, ROWS:], gzx[ROWS:, :], preferred_element_type=F32)
        return jnp.where(group_of == g, term, total_)

    grad_kv = conv[...] + lax.fori_loop(0, GROUPS, back_later, zeros)
    out_k[...] = (grad_kv * values[...].astype(F32)).astype(BF16)
    out_v[...] = (grad_kv * keys[...].astype(F32)).astype(BF16)

    for copy in started:
        copy.wait_send()

    @pl.when(is_home)
    def _():
        for copy in own_out(0) + side_out(0, 0) + side_out(1, 0) + across_out(0):
            copy.wait_send()

    @pl.when(home_half)
    def _():
        pre_copy().wait_send()

    for i in range(1, NY):
        y_copy(i, mod(y - i, NY)).wait_recv()
    final = sums_y[0]
    for i in range(1, NY):
        final = final + sums_y[i]
    out_f[...] = final


def hand_over(*refs):
    for src, dst in zip(refs[:4], refs[4:]):
        dst[...] = src[...]


def per_device(*arrays):
    vmem = pl.BlockSpec(memory_space=pltpu.VMEM)
    dma = pltpu.SemaphoreType.DMA
    results = pl.pallas_call(
        kernel,
        out_shape=(
            pltpu.VMEM((ROWS, WIDE), BF16),
            pltpu.VMEM((ROWS, WIDE), BF16),
            pltpu.VMEM((ROWS, WIDE), BF16),
            pltpu.VMEM((GROUPS, TAPS), F32),
        ),
        in_specs=[pl.BlockSpec(memory_space=pl.ANY)] * 6,
        out_specs=(vmem,) * 4,
        scratch_shapes=[
            pltpu.VMEM((ROWS, WIDE), BF16),
            pltpu.VMEM((ROWS, WIDE), BF16),
            pltpu.VMEM((ROWS, WIDE), BF16),
            pltpu.VMEM((ROWS, WIDE), BF16),
            pltpu.VMEM((GROUPS, TAPS), BF16),
            dma((6,)),
            pltpu.SemaphoreType.REGULAR,
            pltpu.VMEM((NY, NL * ROWS, WIDE), BF16),
            pltpu.VMEM((NY, WIDE, WIDE), BF16),
            pltpu.VMEM((NL - 1, ROWS, WIDE), BF16),
            pltpu.VMEM((NL - 1, ROWS, WIDE), BF16),
            pltpu.VMEM((2 * ROWS, WIDE), BF16),
            pltpu.VMEM((3 * ROWS, WIDE), BF16),
            pltpu.VMEM((2 * ROWS, WIDE), BF16),
            pltpu.VMEM((GROUPS, ROWS, WIDE), BF16),
            pltpu.VMEM((GROUPS, ROWS, WIDE), BF16),
            pltpu.VMEM((ROWS, WIDE), F32),
            pltpu.VMEM((NL, GROUPS, TAPS), F32),
            pltpu.VMEM((NY, GROUPS, TAPS), F32),
            dma((2, 4, 2)), dma((2, 4, 2)), dma, dma, dma((2, 2)), dma((5,)), dma((9,)),
            dma((3, 9)), dma((3, 9)), dma((4, 9)), dma((4, 9)),
            dma((2,)), dma((2,)), dma((NL - 1,)), dma((NL - 1,)),
            dma((NL - 1,)), dma((NL - 1,)), dma((NY - 1,)), dma((NY - 1,)),
        ],
        compiler_params=pltpu.CompilerParams(collective_id=0, has_side_effects=True),
        name="block_backward",
    )(*arrays)
    return pl.pallas_call(
        hand_over,
        out_shape=tuple(jax.ShapeDtypeStruct(a.shape, a.dtype) for a in results),
        in_specs=[vmem] * 4,
        out_specs=(vmem,) * 4,
        name="hand_over",
    )(*[pltpu.with_memory_space_constraint(r, pltpu.VMEM) for r in results])


def solution(mesh):
    here = P("ctx", "fsdp")
    return jax.shard_map(
        per_device,
        mesh=mesh,
        in_specs=(here, here, here, here, P("fsdp", None), here),
        out_specs=(here, here, here, P("fsdp", None)),
        check_vma=False,
    )
```
